128 devices in a mesh: row: 8 (over z, core), col: 16 (over x, y).
Axes of the slice: x: 4, y: 4, z: 4, core: 2. Of those that a mesh axis runs over, the one named last changes fastest.
Arguments:
- obj_re: float32 [4096, 8192], P('row', 'col'), may hold values from -4 to 4
- obj_im: float32 [4096, 8192], P('row', 'col'), may hold values from -4 to 4
- probe_re: float32 [512, 512], replicated, may hold values from -6 to 6
- probe_im: float32 [512, 512], replicated, may hold values from -6 to 6
- amplitude: bfloat16 [8, 64, 512, 512], P('row', 'col'), may hold values from 0.099609375 to 3
- offset_y: int32 [8, 64], P('row', 'col'), may hold values from 0 to 511
- offset_x: int32 [8, 64], P('row', 'col'), may hold values from 0 to 511
- counts: int32 [8, 16], P('row', 'col'), may hold values from 1 to 4, as said below
Outputs:
- new_re: float32 [4096, 8192], P('row', 'col')
- new_im: float32 [4096, 8192], P('row', 'col')
The draws below stay inside these ranges and needn't reach their ends.
Inputs may be any that keep to these rules, and one draw needn't show every extreme that they name: The live slots of a device are its first counts[r, c] slots; some device has 4 live slots. `offset_y`: A window starts inside the tile of the device that holds its slot.
All inputs are finite; a program needn't handle non-finite values.
Results may differ from the reference program's by a relative error of at most 0.0024.
The reference program's roundings to bfloat16 on the way count: a program that leaves them out, or rounds other values in their place, can miss the bound.
Values may be sent and summed in bfloat16 or wider, within the bound.
A program may use at most 128 MiB of HBM per device.

```python
import math
import jax
import jax.numpy as jnp
from jax import lax

P_SIZE = 512
SLOT_DEV = 4
NY = 4096
NX = 8192
SLOT_COLS = 64
N_ROW = 8
N_COL = 16


def draw_counts(key, part):
    first_key, second_key = jax.random.split(jax.random.fold_in(key, 11))
    level = jax.random.randint(first_key, (N_ROW, N_COL), 0, 8)
    live_count = 1 + SLOT_DEV * level * level // 64
    chosen = jax.random.randint(second_key, (), 0, N_ROW * N_COL)
    flat_counts = live_count.reshape(-1)
    flat_counts = jnp.where(jnp.arange(N_ROW * N_COL) == chosen, SLOT_DEV, flat_counts)
    return flat_counts.reshape(N_ROW, N_COL).astype(jnp.int32)


def place_ends(values, rng, least, high):
    longest = values.shape.index(max(values.shape))
    spots = []
    for shift in (0, 1):
        where = [jax.random.randint(jax.random.fold_in(rng, axis), (), 0, length) for axis, length in enumerate(values.shape)]
        where[longest] = (where[longest] + shift) % values.shape[longest]
        spots.append(tuple(where))
    return values.at[spots[0]].set(least).at[spots[1]].set(high)


def block_scale(rng, dims, pieces, smallest, high):
    loudness = 1.0
    for axis_at, shards_of in pieces:
        draws = jax.random.uniform(jax.random.fold_in(jax.random.fold_in(rng, 6), axis_at), (shards_of,), jnp.float32, smallest / len(pieces), high / len(pieces))
        loudness = loudness * jnp.repeat(jnp.exp(draws), dims[axis_at] // shards_of).reshape((-1,) + (1,) * (len(dims) - 1 - axis_at))
    return loudness


def scatter_about(own_key, shape, deviation, bound, pieces=(), kind=jnp.bfloat16):
    values = jax.random.normal(own_key, shape, jnp.float32) * deviation
    if len(pieces) > 0:
        values = block_scale(own_key, shape, pieces, -0.22, 0.18) * values
    return jnp.clip(values, min=-bound, max=bound).astype(kind)


def setup_inputs(seed: int = 0) -> dict:
    splits = jax.random.split(jax.random.key(seed), 9)
    obj_re = scatter_about(splits[0], (NY, NX), 0.5, 4.0, ((0, 8), (1, 16)), jnp.float32)
    obj_im = scatter_about(splits[1], (NY, NX), 0.5, 4.0, ((0, 8), (1, 16)), jnp.float32)
    probe_re = scatter_about(splits[2], (P_SIZE, P_SIZE), 1.0, 6.0, (), jnp.float32)
    probe_im = scatter_about(splits[3], (P_SIZE, P_SIZE), 1.0, 6.0, (), jnp.float32)
    amplitude = jnp.clip(jnp.exp(math.log(3.0) - 3.4051113 * jax.random.uniform(splits[4], (N_ROW, SLOT_COLS, P_SIZE, P_SIZE), jnp.float32) ** block_scale(splits[4], (N_ROW, SLOT_COLS, P_SIZE, P_SIZE), ((0, 8), (1, 16)), -0.2, 0.2)), 0.099609375, 3.0).astype(jnp.bfloat16)
    offset_y = place_ends(jax.random.randint(splits[5], (N_ROW, SLOT_COLS), 0, P_SIZE), jax.random.fold_in(splits[5], 1), 0, P_SIZE - 1).astype(jnp.int32)
    offset_x = place_ends(jax.random.randint(splits[6], (N_ROW, SLOT_COLS), 0, P_SIZE), jax.random.fold_in(splits[6], 1), 0, P_SIZE - 1).astype(jnp.int32)
    counts = draw_counts(jax.random.fold_in(splits[8], 71), 0)
    return dict(obj_re=obj_re, obj_im=obj_im, probe_re=probe_re, probe_im=probe_im, amplitude=amplitude, offset_y=offset_y, offset_x=offset_x, counts=counts)


modulus_floor = 0.5
shrink_level = 0.2
step_size = 0.5
epsilon = 1e-05

def dft_tables(pattern_side):
    ordinal = jnp.arange(pattern_side, dtype=jnp.int32)
    phase_index = ordinal[:, None] * ordinal[None, :] % pattern_side
    angles = phase_index.astype(jnp.float32) * (2.0 * math.pi / pattern_side)
    norming = 1.0 / math.sqrt(pattern_side)
    return ((jnp.cos(angles) * norming).astype(jnp.bfloat16), (-jnp.sin(angles) * norming).astype(jnp.bfloat16))

def matmul(left_op, right_op):
    return jnp.dot(left_op, right_op, preferred_element_type=jnp.float32)

def spectrum_rows(patch_tile, probe_re, probe_im, cos_table, sin_table):
    object_re = patch_tile[0].astype(jnp.float32)
    object_im = patch_tile[1].astype(jnp.float32)
    exit_re = (probe_re * object_re - probe_im * object_im).astype(jnp.bfloat16)
    exit_im = (probe_re * object_im + probe_im * object_re).astype(jnp.bfloat16)
    half_re = matmul(cos_table, exit_re) - matmul(sin_table, exit_im)
    half_im = matmul(cos_table, exit_im) + matmul(sin_table, exit_re)
    return jnp.stack([half_re, half_im]).astype(jnp.bfloat16)

def correct_rows(half_spec, measured, cos_table, sin_table):
    spec_re = matmul(half_spec[0], cos_table) - matmul(half_spec[1], sin_table)
    spec_im = matmul(half_spec[0], sin_table) + matmul(half_spec[1], cos_table)
    modulus = jnp.sqrt(spec_re * spec_re + spec_im * spec_im)
    factor = measured.astype(jnp.float32) / jnp.maximum(modulus, modulus_floor) - 1.0
    delta_re = (spec_re * factor).astype(jnp.bfloat16)
    delta_im = (spec_im * factor).astype(jnp.bfloat16)
    back_re = matmul(delta_re, cos_table) + matmul(delta_im, sin_table)
    back_im = matmul(delta_im, cos_table) - matmul(delta_re, sin_table)
    return jnp.stack([back_re, back_im]).astype(jnp.bfloat16)

def object_term(partial_back, probe_re, probe_im, cos_table, sin_table):
    wave_re = matmul(cos_table, partial_back[0]) + matmul(sin_table, partial_back[1])
    wave_im = matmul(cos_table, partial_back[1]) - matmul(sin_table, partial_back[0])
    return jnp.stack([probe_re * wave_re + probe_im * wave_im, probe_re * wave_im - probe_im * wave_re])

def shrink(entries):
    return entries - jnp.clip(entries, -shrink_level, shrink_level)

def haar_clean(field):
    top_left = field[:, 0::2, 0::2]
    top_right = field[:, 0::2, 1::2]
    low_left = field[:, 1::2, 0::2]
    low_right = field[:, 1::2, 1::2]
    coarse = 0.5 * (top_left + top_right + low_left + low_right)
    across = shrink(0.5 * (top_left - top_right + low_left - low_right))
    downward = shrink(0.5 * (top_left + top_right - low_left - low_right))
    diagonal = shrink(0.5 * (top_left - top_right - low_left + low_right))
    new_top_left = 0.5 * (coarse + across + downward + diagonal)
    new_top_right = 0.5 * (coarse - across + downward - diagonal)
    new_low_left = 0.5 * (coarse + across - downward - diagonal)
    new_low_right = 0.5 * (coarse - across - downward + diagonal)
    planes, height, breadth = top_left.shape
    top_rows = jnp.stack([new_top_left, new_top_right], axis=-1).reshape(planes, height, 2 * breadth)
    bottom_rows = jnp.stack([new_low_left, new_low_right], axis=-1).reshape(planes, height, 2 * breadth)
    return jnp.stack([top_rows, bottom_rows], axis=2).reshape(planes, 2 * height, 2 * breadth)

def reference(obj_re, obj_im, probe_re, probe_im, amplitude, offset_y, offset_x, counts):
    cos_table, sin_table = dft_tables(P_SIZE)
    probe_power = jnp.mean(probe_re * probe_re + probe_im * probe_im) + epsilon
    object_bf = jnp.stack([obj_re, obj_im]).astype(jnp.bfloat16)
    wrapped = jnp.concatenate([object_bf, object_bf[:, :P_SIZE, :]], axis=1)
    wrapped = jnp.concatenate([wrapped, wrapped[:, :, :P_SIZE]], axis=2)
    anchor = jnp.int32(0)
    row_slots = N_COL * SLOT_DEV

    def add_slot(counter, accumulated):
        counter = jnp.asarray(counter).astype(jnp.int32)
        tile_row = counter // row_slots
        slot_col = counter % row_slots
        tile_col = slot_col // SLOT_DEV
        slot_index = slot_col % SLOT_DEV
        row_at = (tile_row * P_SIZE + offset_y[tile_row, slot_col]).astype(jnp.int32)
        col_at = (tile_col * P_SIZE + offset_x[tile_row, slot_col]).astype(jnp.int32)

        def process(current):
            patch_tile = lax.dynamic_slice(wrapped, (anchor, row_at, col_at), (2, P_SIZE, P_SIZE))
            half_spec = spectrum_rows(patch_tile, probe_re, probe_im, cos_table, sin_table)
            partial_back = correct_rows(half_spec, amplitude[tile_row, slot_col], cos_table, sin_table)
            update = object_term(partial_back, probe_re, probe_im, cos_table, sin_table)
            window = lax.dynamic_slice(current, (anchor, row_at, col_at), (2, P_SIZE, P_SIZE))
            return lax.dynamic_update_slice(current, window + update, (anchor, row_at, col_at))

        def unchanged(current):
            return current
        return lax.cond(slot_index < counts[tile_row, tile_col], process, unchanged, accumulated)
    accumulated = lax.fori_loop(0, N_ROW * row_slots, add_slot, jnp.zeros((2, NY + P_SIZE, NX + P_SIZE), jnp.float32))
    intersection = accumulated[:, :NY, :NX]
    intersection = intersection.at[:, :P_SIZE, :].add(accumulated[:, NY:, :NX])
    intersection = intersection.at[:, :, :P_SIZE].add(accumulated[:, :NY, NX:])
    intersection = intersection.at[:, :P_SIZE, :P_SIZE].add(accumulated[:, NY:, NX:])
    half_step = jnp.stack([obj_re, obj_im]) + step_size / probe_power * intersection
    shifted = jnp.roll(half_step, (-1, -1), axis=(1, 2))
    cleaned = 0.5 * (haar_clean(half_step) + jnp.roll(haar_clean(shifted), (1, 1), axis=(1, 2)))
    return (cleaned[0], cleaned[1])
```

```python
import math

import jax
import jax.numpy as jnp
import ml_dtypes
import numpy as np
from jax import lax
from jax.experimental import pallas as pl
from jax.experimental.pallas import tpu as pltpu
from jax.sharding import PartitionSpec as P

SIDE = 512
QUARTER = 128
HALF = 256
SLOTS = 4
EPS = 1e-05
STEP = 0.5
SHRINK = 0.2
BF = jnp.bfloat16
F32 = jnp.float32
MESH = pl.DeviceIdType.MESH


def tables():
    phase = np.arange(SIDE) * (2.0 * math.pi / SIDE)
    norming = 1.0 / math.sqrt(SIDE)
    cosine = (np.cos(phase) * norming).astype(np.float32)
    sine = (-np.sin(phase) * norming).astype(np.float32)
    quarter = np.arange(4) * QUARTER
    cosine[quarter[1::2]] = 0.0
    sine[quarter[0::2]] = 0.0

    def entries(rows, cols):
        at = np.outer(rows, cols) % SIDE
        return cosine[at], sine[at]

    natural = np.arange(SIDE)
    by_class = np.concatenate([natural[m::4] for m in range(4)])
    block = np.concatenate([np.arange(m, QUARTER, 4) for m in range(4)])
    even, odd = np.arange(0, HALF, 2), np.arange(1, HALF, 2)
    minus_even = (SIDE - even) % SIDE
    minus_even[0] = HALF
    freq = np.concatenate([even, odd, minus_even, SIDE - odd])
    c, s = entries(block, by_class)
    first = np.concatenate([c, s], axis=0)
    c, s = entries(natural, freq[:HALF])
    s[:, 0] = entries(natural, np.array([HALF]))[0][:, 0]
    second = np.concatenate([c, s], axis=1)
    c, s = entries(freq, natural)
    third = np.concatenate([c, s], axis=0)
    c, s = entries(natural, by_class)
    fourth = np.concatenate([c, s], axis=1)
    return [t.astype(ml_dtypes.bfloat16) for t in (first, second, third, fourth)]


def dot(a, b):
    return jnp.dot(a, b, preferred_element_type=F32)


def iota(shape, dim):
    return lax.broadcasted_iota(jnp.int32, shape, dim)


def strided(ref, p, start, size):
    return jnp.concatenate([ref[p, k, pl.ds(start, size, stride=4), :] for k in range(4)], axis=1)


def one_hot(hit):
    return jnp.where(hit, 1.0, 0.0).astype(BF)


def kernel(offy, offx, cnt, objr, obji, prbr, prbi, amp, b1h, b2h, b3h, b4h,
           outr, outi,
           objn, tile, prbn, prot, ampr, ampp, b1, b2, b3, b4,
           t1, t2, t3, t4, gbuf, half, back, dbuf, term,
           slr, sur, sll, rlr, rll, rur, hs, ext, res, outn,
           msg, halo, colt, power,
           insem, outsem, fs, fr, bs, br, hsem, hrem):
    nr, nc = lax.axis_size("row"), lax.axis_size("col")
    r, c = lax.axis_index("row"), lax.axis_index("col")
    up, down = lax.rem(r + nr - 1, nr), lax.rem(r + 1, nr)
    left, right = lax.rem(c + nc - 1, nc), lax.rem(c + 1, nc)

    moves = []
    for ref, dst, p in ((objr, objn, 0), (obji, objn, 1), (prbr, prbn, 0), (prbi, prbn, 1)):
        moves += [(ref.at[:, k * QUARTER:(k + 1) * QUARTER], dst.at[p, k]) for k in range(4)]
    moves += [(amp.at[0], ampr), (b1h, b1), (b2h, b2), (b3h, b3), (b4h, b4)]
    ins = [pltpu.make_async_copy(a, b, insem.at[i]) for i, (a, b) in enumerate(moves)]
    for copy in ins:
        copy.start()

    barrier = pltpu.get_barrier_semaphore()
    for rr in (up, r, down):
        for cc in (left, c, right):
            if rr is r and cc is c:
                continue
            pl.semaphore_signal(barrier, inc=1, device_id=(rr, cc), device_id_type=MESH)

    def remote(src, dst, ssem, rsem, rr, cc):
        return pltpu.make_async_remote_copy(src_ref=src, dst_ref=dst, send_sem=ssem, recv_sem=rsem,
                                            device_id=(rr, cc), device_id_type=MESH)

    def to_left(p, m):
        return remote(tile.at[0, p, m], tile.at[1, p, m], fs.at[0, p, m], fr.at[0, p, m], r, left)

    def to_up(p, m):
        return remote(tile.at[0, p, m], tile.at[2, p, m], fs.at[1, p, m], fr.at[1, p, m], up, c)

    def pass_up(p, m):
        return remote(tile.at[1, p, m], tile.at[3, p, m], fs.at[2, p, m], fr.at[2, p, m], up, c)

    chunks = [(p, m) for p in range(2) for m in range(4)]
    for p in range(2):
        for copy in ins[4 * p:4 * p + 4]:
            copy.wait()
        for m in range(4):
            tile[0, p, m] = strided(objn, p, m, QUARTER).astype(BF)
            if p == 0 and m == 0:
                pl.semaphore_wait(barrier, 8)
            to_left(p, m).start()
            to_up(p, m).start()
    for copy in ins[8:]:
        copy.wait()

    total = jnp.zeros((8, SIDE), F32)
    for p in range(2):
        def add(i, acc, p=p):
            x = jnp.concatenate([prbn[p, k, pl.ds(pl.multiple_of(i * 8, 8), 8), :] for k in range(4)], axis=1)
            return acc + x * x
        total = lax.fori_loop(0, SIDE // 8, add, total)
    mean = jnp.sum(jnp.sum(total, axis=1, keepdims=True), axis=0, keepdims=True) * (1.0 / (SIDE * SIDE)) + EPS
    power[...] = jnp.broadcast_to(STEP / mean, (8, QUARTER))

    def prepare(s):
        oy, ox = offy[0, s], offx[0, s]
        live = jnp.where(s < cnt[0, 0], 1.0, 0.0).astype(F32)
        lam, freq = iota((SIDE, SIDE), 1), iota((SIDE, SIDE), 0)
        lane = lam & 127
        even_minus = jnp.where(lane == 0, HALF, SIDE - 2 * lane)
        want = jnp.where(lam < 128, 2 * lane,
                         jnp.where(lam < 256, 2 * lane + 1,
                                   jnp.where(lam < 384, even_minus, SIDE - 1 - 2 * lane)))
        mixed = dot(ampr[s], one_hot(freq == want)).astype(BF)
        pick = one_hot(lam == 4 * (freq & 127) + (freq >> 7))
        ampp[s] = dot(pick, mixed).astype(BF).reshape(4, QUARTER, SIDE)
        for m in range(4):
            turn = lax.shift_right_logical(oy + m, 2) & 127
            for p in range(2):
                x = strided(prbn, p, m, QUARTER) * live
                prot[s, p, m] = pltpu.roll(pltpu.roll(x, turn, 0), ox, 1)
            cs = pltpu.roll(b1[:, m * QUARTER:(m + 1) * QUARTER].astype(F32), turn, 1)
            cc, ss = cs[:QUARTER], cs[QUARTER:]
            t1[s, m] = jnp.concatenate([jnp.concatenate([cc, -ss], axis=1),
                                        jnp.concatenate([ss, cc], axis=1)], axis=0).astype(BF)
        rows, cols = iota((SIDE, SIDE), 0), iota((SIDE, SIDE), 1)
        t2[s] = dot(one_hot(cols == ((rows - ox) & 511)), b2[...]).astype(BF)
        rows, cols = iota((SIDE, HALF), 0), iota((SIDE, HALF), 1)
        cs = dot(b3[...], one_hot(rows == ((cols - ox) & 511)))
        for par in range(2):
            a = par * QUARTER
            cc = jnp.concatenate([cs[a:a + 128], cs[a + 256:a + 384]], axis=0)
            ss = jnp.concatenate([cs[a + 512:a + 640], cs[a + 768:a + 896]], axis=0)
            t3[s, par] = jnp.concatenate([jnp.concatenate([cc, -ss], axis=1),
                                          jnp.concatenate([ss, cc], axis=1)], axis=0).astype(BF)
        rows, cols = iota((QUARTER, SIDE), 0), iota((QUARTER, SIDE), 1)
        place = 4 * (rows & 31) + lax.shift_right_logical(rows, 5)
        cs = dot(one_hot(cols == ((place - oy) & 511)), b4[...])
        for m in range(4):
            cc = cs[:, m * QUARTER:(m + 1) * QUARTER]
            ss = cs[:, SIDE + m * QUARTER:SIDE + (m + 1) * QUARTER]
            t4[s, m] = jnp.concatenate([jnp.concatenate([cc, ss], axis=1),
                                        jnp.concatenate([-ss, cc], axis=1)], axis=0).astype(BF)

    def prepare_and_pass(s, carry):
        prepare(s)
        p, m = s // 2, 2 * (s % 2)
        for k in range(2):
            to_left(p, m + k).wait_recv()
            pass_up(p, m + k).start()
        return carry

    lax.fori_loop(0, SLOTS, prepare_and_pass, 0)
    for p, m in chunks:
        to_up(p, m).wait_recv()
    for p, m in chunks:
        pass_up(p, m).wait_recv()

    def one_slot(s, carry):
        oy, ox = offy[0, s], offx[0, s]
        for h in range(2):
            cols = slice(h * HALF, (h + 1) * HALF)
            for m in range(4):
                mu = (m + oy) & 3
                xs = []
                for i in range(0, QUARTER, 32):
                    rs = slice(i, i + 32)
                    own_row = 4 * (iota((32, HALF), 0) + i) + mu >= oy
                    own_col = iota((32, HALF), 1) + h * HALF >= ox
                    part = []
                    for p in range(2):
                        q = [tile[k, p, mu, rs, cols].astype(F32) for k in range(4)]
                        part.append(jnp.where(own_row, jnp.where(own_col, q[0], q[1]),
                                              jnp.where(own_col, q[2], q[3])))
                    pr, pi = prot[s, 0, m, rs, cols], prot[s, 1, m, rs, cols]
                    xs.append(((pr * part[0] - pi * part[1]).astype(BF), (pr * part[1] + pi * part[0]).astype(BF)))
                x = jnp.concatenate([a for a, _ in xs] + [b for _, b in xs], axis=0)
                gbuf[m] = dot(t1[s, m], x)
            for i in range(0, QUARTER, 32):
                re, im = slice(i, i + 32), slice(QUARTER + i, QUARTER + i + 32)
                g = [(gbuf[m, re, :], gbuf[m, im, :]) for m in range(4)]
                ar, ai = g[0][0] + g[2][0], g[0][1] + g[2][1]
                br_, bi_ = g[0][0] - g[2][0], g[0][1] - g[2][1]
                cr, ci = g[1][0] + g[3][0], g[1][1] + g[3][1]
                dr, di = g[1][0] - g[3][0], g[1][1] - g[3][1]
                mm = i // 32
                for q, (xr, xi) in enumerate([(ar + cr, ai + ci), (br_ + di, bi_ - dr),
                                              (ar - cr, ai - ci), (br_ - di, bi_ + dr)]):
                    half[0, mm, q * 32:(q + 1) * 32, cols] = xr.astype(BF)
                    half[1, mm, q * 32:(q + 1) * 32, cols] = xi.astype(BF)
        for m in range(4):
            prod = dot(jnp.concatenate([half[0, m], half[1, m]], axis=0), t2[s])
            gbuf[0, :, :] = prod[:, :HALF]
            gbuf[1, :, :] = prod[:, HALF:]
            for i in range(0, QUARTER, 32):
                re, im = slice(i, i + 32), slice(QUARTER + i, QUARTER + i + 32)
                for par in range(2):
                    ln = slice(par * 128, par * 128 + 128)
                    rc, ic = gbuf[0, re, ln], gbuf[0, im, ln]
                    rs_, is_ = gbuf[1, re, ln], gbuf[1, im, ln]
                    pr_, pi_ = rc - is_, ic + rs_
                    mr_, mi_ = rc + is_, ic - rs_
                    if par == 0:
                        first = iota((32, QUARTER), 1) == 0
                        pr_, pi_ = jnp.where(first, rc, pr_), jnp.where(first, ic, pi_)
                        mr_, mi_ = jnp.where(first, rs_, mr_), jnp.where(first, is_, mi_)
                    for k, (a, b) in enumerate([(pr_, pi_), (mr_, mi_)]):
                        tt = 2 * k + par
                        mag = ampp[s, m, i:i + 32, tt * 128:(tt + 1) * 128].astype(F32)
                        factor = mag * lax.rsqrt(jnp.maximum(a * a + b * b, 0.25)) - 1.0
                        dbuf[par, i:i + 32, k * 128:(k + 1) * 128] = (a * factor).astype(BF)
                        dbuf[par, i:i + 32, 256 + k * 128:256 + (k + 1) * 128] = (b * factor).astype(BF)
            e = dot(dbuf[0], t3[s, 0])
            o = dot(dbuf[1], t3[s, 1])
            a, b = e + o, e - o
            back[0, m, :, :HALF] = a[:, :HALF].astype(BF)
            back[1, m, :, :HALF] = a[:, HALF:].astype(BF)
            back[0, m, :, HALF:] = b[:, :HALF].astype(BF)
            back[1, m, :, HALF:] = b[:, HALF:].astype(BF)
        for h in range(2):
            cols = slice(h * HALF, (h + 1) * HALF)
            for m in range(4):
                gbuf[m] = dot(t4[s, m], jnp.concatenate([back[0, m, :, cols], back[1, m, :, cols]], axis=0))
            for i in range(0, QUARTER, 32):
                re, im = slice(i, i + 32), slice(QUARTER + i, QUARTER + i + 32)
                g = [(gbuf[m, re, :], gbuf[m, im, :]) for m in range(4)]
                ar, ai = g[0][0] + g[2][0], g[0][1] + g[2][1]
                br_, bi_ = g[0][0] - g[2][0], g[0][1] - g[2][1]
                cr, ci = g[1][0] + g[3][0], g[1][1] + g[3][1]
                dr, di = g[1][0] - g[3][0], g[1][1] - g[3][1]
                mu = i // 32
                m = (mu - oy) & 3
                for q, (wr, wi) in enumerate([(ar + cr, ai + ci), (br_ - di, bi_ + dr),
                                              (ar - cr, ai - ci), (br_ + di, bi_ - dr)]):
                    rs = slice(q * 32, (q + 1) * 32)
                    pr, pi = prot[s, 0, m, rs, cols], prot[s, 1, m, rs, cols]
                    term[s, 0, mu, rs, cols] = pr * wr + pi * wi
                    term[s, 1, mu, rs, cols] = pr * wi - pi * wr
        return carry

    lax.fori_loop(0, SLOTS, one_slot, 0)

    def down_right(p, m):
        return remote(slr.at[p, m], rlr.at[p, m], bs.at[0, p, m], br.at[0, p, m], down, c)

    def down_left(p, m):
        return remote(sll.at[p, m], rll.at[p, m], bs.at[1, p, m], br.at[1, p, m], down, c)

    def to_right(p, m):
        return remote(sur.at[p, m], rur.at[p, m], bs.at[2, p, m], br.at[2, p, m], r, right)

    for p, m in chunks:
        def gather(i, carry, p=p, m=m):
            rs = pl.ds(pl.multiple_of(i * 16, 16), 16)
            rows = 4 * (iota((16, SIDE), 0) + i * 16) + m
            lanes = iota((16, SIDE), 1)
            al = jnp.zeros((16, SIDE), F32)
            ur, ll, lr = al, al, al
            zero = al
            for s in range(SLOTS):
                x = term[s, p, m, rs, :]
                own_row, own_col = rows >= offy[0, s], lanes >= offx[0, s]
                u = jnp.where(own_row, x, zero)
                l = jnp.where(own_row, zero, x)
                al = al + jnp.where(own_col, u, zero)
                ur = ur + jnp.where(own_col, zero, u)
                ll = ll + jnp.where(own_col, l, zero)
                lr = lr + jnp.where(own_col, zero, l)
            hs[p, m, rs, :] = al
            term[0, p, m, rs, :] = ur
            sll[p, m, rs, :] = ll.astype(BF)
            slr[p, m, rs, :] = lr.astype(BF)
            return carry
        lax.fori_loop(0, QUARTER // 16, gather, 0)
        down_right(p, m).start()
    for p, m in chunks:
        down_left(p, m).start()
    for p, m in chunks:
        down_right(p, m).wait_recv()

        def add_right(i, carry, p=p, m=m):
            rs = pl.ds(pl.multiple_of(i * 16, 16), 16)
            sur[p, m, rs, :] = (term[0, p, m, rs, :] + rlr[p, m, rs, :].astype(F32)).astype(BF)
            return carry
        lax.fori_loop(0, QUARTER // 16, add_right, 0)
        to_right(p, m).start()
    for p, m in chunks:
        down_left(p, m).wait_recv()
        to_right(p, m).wait_recv()
        scale = power[0:1, 0:1]
        for i in range(0, QUARTER, 16):
            rs = slice(i, i + 16)
            sums = hs[p, m, rs, :] + (rll[p, m, rs, :].astype(F32) + rur[p, m, rs, :].astype(F32))
            hs[p, m, rs, :] = strided(objn, p, m + 4 * i, 16) + scale * sums

    lane = iota((QUARTER, QUARTER), 1)
    cols = jnp.zeros((QUARTER, QUARTER), F32)
    for p, m in chunks:
        at = 4 * p + m
        cols = jnp.where(lane == at, pltpu.roll(hs[p, m, :, 0:QUARTER], at, 1), cols)
        cols = jnp.where(lane == 8 + at, pltpu.roll(hs[p, m, :, SIDE - QUARTER:], (8 + at + 1) % QUARTER, 1), cols)
    turned = cols.T
    msg[2] = turned[0:8]
    msg[3] = turned[8:16]
    for p in range(2):
        for k in range(4):
            msg[0, 4 * p + k:4 * p + k + 1, :] = hs[p, 0, 0:1, k * 128:(k + 1) * 128]
            msg[1, 4 * p + k:4 * p + k + 1, :] = hs[p, 3, 127:128, k * 128:(k + 1) * 128]
    plan = [(0, 2, up, left), (0, 1, up, c), (0, 0, up, right),
            (1, 5, down, left), (1, 4, down, c), (1, 3, down, right),
            (2, 6, r, left), (3, 7, r, right)]
    rims = [remote(msg.at[a], halo.at[b], hsem.at[i], hrem.at[i], rr, cc) for i, (a, b, rr, cc) in enumerate(plan)]
    for copy in rims:
        copy.start()
    for copy in rims:
        copy.wait_recv()
    filler = jnp.zeros((QUARTER - 8, QUARTER), F32)
    for k in range(2):
        colt[k, 0:QUARTER, :] = jnp.concatenate([halo[6 + k], filler], axis=0).T

    lane8 = iota((8, QUARTER), 1)
    for k, (src, tl, ln) in enumerate([(2, 0, 0), (0, 3, 127)]):
        row = jnp.zeros((8, QUARTER), F32)
        for p in range(2):
            v = jnp.broadcast_to(halo[src, 4 * p + tl:4 * p + tl + 1, :], (8, QUARTER))
            row = jnp.where(lane8 == 4 * p, pltpu.roll(v, (4 * p - ln) % QUARTER, 1), row)
        colt[k, QUARTER:QUARTER + 8, :] = row

    def out_copy(p, k):
        return pltpu.make_async_copy(outn.at[p, k], (outr, outi)[p].at[:, k * QUARTER:(k + 1) * QUARTER], outsem.at[p, k])

    def partner(x, lanes_odd, shifted, xr=None, xl=None):
        ahead, behind = pltpu.roll(x, SIDE - 1, 1), pltpu.roll(x, 1, 1)
        if not shifted:
            return jnp.where(lanes_odd, behind, ahead)
        q = jnp.where(lanes_odd, ahead, behind)
        ln = iota((x.shape[0], QUARTER), 1)
        return jnp.concatenate([jnp.where(ln == 0, xl, q[:, :128]), q[:, 128:384],
                                jnp.where(ln == 127, xr, q[:, 384:])], axis=1)

    def clipped(x):
        return x - jnp.clip(x, -2 * SHRINK, 2 * SHRINK)

    def clean(a, b, shifted, ar=None, br_=None, al=None, bl=None):
        odd = (iota(a.shape, 1) & 1) == 1
        s, d = a + b, a - b
        if shifted:
            ps = partner(s, odd, True, ar + br_, al + bl)
            pd = partner(d, odd, True, ar - br_, al - bl)
        else:
            ps, pd = partner(s, odd, False), partner(d, odd, False)
        x = (s + ps) + clipped(s - ps)
        y = clipped(d + pd) + clipped(d - pd)
        return x + y, x - y

    for p in range(2):
        ext[0:QUARTER, :] = hs[p, 0]
        for k in range(4):
            ext[QUARTER:QUARTER + 1, k * 128:(k + 1) * 128] = halo[1, 4 * p + k:4 * p + k + 1, :]

        def at_right(rs, m):
            return pltpu.roll(colt[0, rs, :], (127 - (4 * p + m)) % QUARTER, 1)

        def at_left(rs, m):
            return pltpu.roll(colt[1, rs, :], (QUARTER - (4 * p + m)) % QUARTER, 1)

        above = jnp.concatenate([halo[4, 4 * p + k:4 * p + k + 1, :] for k in range(4)], axis=1)
        corner_l = pltpu.roll(jnp.broadcast_to(halo[3, 4 * p + 3:4 * p + 4, :], (8, QUARTER)), 1, 1)
        corner_r = pltpu.roll(jnp.broadcast_to(halo[5, 4 * p:4 * p + 1, :], (8, QUARTER)), 127, 1)
        eight = slice(0, 8)
        _, top = clean(jnp.broadcast_to(above, (8, SIDE)), hs[p, 0, eight, :], True,
                       corner_r, at_right(eight, 0), corner_l, at_left(eight, 0))
        res[0:1, :] = top[0:1, :]
        for i in range(0, QUARTER, 16):
            rs, nx = slice(i, i + 16), slice(i + 1, i + 17)
            x, y = clean(hs[p, 3, rs, :], ext[nx, :], True,
                         at_right(rs, 3), at_right(nx, 0), at_left(rs, 3), at_left(nx, 0))
            res[nx, :] = y
            term[1, 0, 3, rs, :] = x
        for i in range(0, QUARTER, 16):
            rs = slice(i, i + 16)
            x1, x2 = clean(hs[p, 1, rs, :], hs[p, 2, rs, :], True,
                           at_right(rs, 1), at_right(rs, 2), at_left(rs, 1), at_left(rs, 2))
            h0, h1 = clean(hs[p, 0, rs, :], hs[p, 1, rs, :], False)
            h2, h3 = clean(hs[p, 2, rs, :], hs[p, 3, rs, :], False)
            outs = [h0 + res[rs, :], h1 + x1, h2 + x2, h3 + term[1, 0, 3, rs, :]]
            for m in range(4):
                for k in range(4):
                    outn[p, k, pl.ds(m + 4 * i, 16, stride=4), :] = 0.125 * outs[m][:, k * 128:(k + 1) * 128]
        for k in range(4):
            out_copy(p, k).start()
    for p in range(2):
        for k in range(4):
            out_copy(p, k).wait()
    for p, m in chunks:
        for copy in (to_left(p, m), to_up(p, m), pass_up(p, m), down_right(p, m), down_left(p, m), to_right(p, m)):
            copy.wait_send()
    for copy in rims:
        copy.wait_send()


def body(obj_re, obj_im, probe_re, probe_im, amplitude, offset_y, offset_x, counts):
    plane = (SIDE, SIDE)
    classes = (4, QUARTER, SIDE)
    split = (2, 4, SIDE, QUARTER)
    vm = pltpu.VMEM
    scratch = [
        vm(split, F32), vm((4, 2) + classes, BF), vm(split, F32), vm((SLOTS, 2) + classes, F32),
        vm((SLOTS,) + plane, BF), vm((SLOTS,) + classes, BF),
        vm((HALF, SIDE), BF), vm(plane, BF), vm((2 * SIDE, SIDE), BF), vm((SIDE, 2 * SIDE), BF),
        vm((SLOTS, 4, HALF, HALF), BF), vm((SLOTS,) + plane, BF), vm((SLOTS, 2) + plane, BF), vm((SLOTS, 4, HALF, HALF), BF),
        vm((4, HALF, HALF), F32), vm((2,) + classes, BF), vm((2,) + classes, BF), vm((2, QUARTER, SIDE), BF),
        vm((SLOTS, 2) + classes, F32),
    ] + [vm((2,) + classes, BF)] * 6 + [
        vm((2,) + classes, F32), vm((QUARTER + 8, SIDE), F32), vm((QUARTER + 8, SIDE), F32), vm(split, F32),
        vm((4, 8, QUARTER), F32), vm((8, 8, QUARTER), F32), vm((2, QUARTER + 8, QUARTER), F32), vm((8, QUARTER), F32),
        pltpu.SemaphoreType.DMA((21,)), pltpu.SemaphoreType.DMA((2, 4)),
    ] + [pltpu.SemaphoreType.DMA((3, 2, 4))] * 4 + [pltpu.SemaphoreType.DMA((8,))] * 2
    smem = pl.BlockSpec(memory_space=pltpu.SMEM)
    anyw = pl.BlockSpec(memory_space=pl.ANY)
    return pl.pallas_call(
        kernel,
        out_shape=(jax.ShapeDtypeStruct(plane, F32),) * 2,
        in_specs=[smem] * 3 + [anyw] * 9,
        out_specs=(anyw, anyw),
        scratch_shapes=scratch,
        compiler_params=pltpu.CompilerParams(collective_id=0, has_side_effects=True, vmem_limit_bytes=62 << 20),
    )(offset_y, offset_x, counts, obj_re, obj_im, probe_re, probe_im, amplitude, *[jnp.asarray(t) for t in tables()])


def solution(mesh):
    return jax.shard_map(
        body,
        mesh=mesh,
        in_specs=(P("row", "col"), P("row", "col"), P(), P(), P("row", "col", None, None),
                  P("row", "col"), P("row", "col"), P("row", "col")),
        out_specs=(P("row", "col"), P("row", "col")),
        check_vma=False,
    )
```

```python
import math

import jax
import jax.numpy as jnp
import ml_dtypes
import numpy as np
from jax import lax
from jax.experimental import pallas as pl
from jax.experimental.pallas import tpu as pltpu
from jax.sharding import PartitionSpec as P

SIDE = 512
QUARTER = 128
HALF = 256
SLOTS = 4
EPS = 1e-05
STEP = 0.5
SHRINK = 0.2
BF = jnp.bfloat16
F32 = jnp.float32
MESH = pl.DeviceIdType.MESH


def tables():
    phase = np.arange(SIDE) * (2.0 * math.pi / SIDE)
    norming = 1.0 / math.sqrt(SIDE)
    cosine = (np.cos(phase) * norming).astype(np.float32)
    sine = (-np.sin(phase) * norming).astype(np.float32)
    quarter = np.arange(4) * QUARTER
    cosine[quarter[1::2]] = 0.0
    sine[quarter[0::2]] = 0.0

    def entries(rows, cols):
        at = np.outer(rows, cols) % SIDE
        return cosine[at], sine[at]

    natural = np.arange(SIDE)
    by_class = np.concatenate([natural[m::4] for m in range(4)])
    block = np.concatenate([np.arange(m, QUARTER, 4) for m in range(4)])
    even, odd = np.arange(0, HALF, 2), np.arange(1, HALF, 2)
    minus_even = (SIDE - even) % SIDE
    minus_even[0] = HALF
    freq = np.concatenate([even, odd, minus_even, SIDE - odd])
    c, s = entries(block, by_class)
    first = np.concatenate([c, s], axis=0)
    c, s = entries(natural, freq[:HALF])
    s[:, 0] = entries(natural, np.array([HALF]))[0][:, 0]
    second = np.concatenate([c, s], axis=1)
    c, s = entries(freq, natural)
    third = np.concatenate([c, s], axis=0)
    c, s = entries(natural, by_class)
    fourth = np.concatenate([c, s], axis=1)
    return [t.astype(ml_dtypes.bfloat16) for t in (first, second, third, fourth)]


def dot(a, b):
    return jnp.dot(a, b, preferred_element_type=F32)


def iota(shape, dim):
    return lax.broadcasted_iota(jnp.int32, shape, dim)


def strided(ref, p, start, size):
    return jnp.concatenate([ref[p, k, pl.ds(start, size, stride=4), :] for k in range(4)], axis=1)


def one_hot(hit):
    return jnp.where(hit, 1.0, 0.0).astype(BF)


ORDER = (0, 3, 1, 2)
BLOCKS = (0, 3, 2, 1)


def butterfly(g, sign):
    ar, ai = g[0][0] + g[2][0], g[0][1] + g[2][1]
    br, bi = g[0][0] - g[2][0], g[0][1] - g[2][1]
    cr, ci = g[1][0] + g[3][0], g[1][1] + g[3][1]
    dr, di = g[1][0] - g[3][0], g[1][1] - g[3][1]
    one = (br - di, bi + dr)
    three = (br + di, bi - dr)
    if sign < 0:
        one, three = three, one
    return [(ar + cr, ai + ci), one, (ar - cr, ai - ci), three]


def kernel(offy, offx, cnt, objr, obji, prbr, prbi, amp, b1h, b2h, b3h, b4h,
           hs, rim,
           objn, tile0, tile1, tile2, tile3, prbn, prot, ampr, ampp, b1, b2, b3, b4,
           t1, t2, t3, t4, gbuf, gtwo, hb, dbuf, term,
           slr, sur, sll, rlr, rll, rur, urf,
           msg, halo, side, beside, power,
           insem, fs, fr, bs, br, hsem, hrem):
    tile = (tile0, tile1, tile2, tile3)
    nr, nc = lax.axis_size("row"), lax.axis_size("col")
    r, c = lax.axis_index("row"), lax.axis_index("col")
    up, down = lax.rem(r + nr - 1, nr), lax.rem(r + 1, nr)
    left, right = lax.rem(c + nc - 1, nc), lax.rem(c + 1, nc)

    moves = []
    for pair, dst in (((objr, obji), objn), ((prbr, prbi), prbn)):
        moves += [(pair[p].at[:, k * QUARTER:(k + 1) * QUARTER], dst.at[p, k]) for k in range(4) for p in range(2)]
    moves += [(b1h, b1), (amp.at[0], ampr), (b2h, b2), (b3h, b3), (b4h, b4)]
    ins = [pltpu.make_async_copy(a, b, insem.at[i]) for i, (a, b) in enumerate(moves)]
    for copy in ins:
        copy.start()

    barrier = pltpu.get_barrier_semaphore()
    for rr, cc in ((up, c), (down, c), (r, left), (r, right)):
        pl.semaphore_signal(barrier, inc=1, device_id=(rr, cc), device_id_type=MESH)

    def remote(src, dst, ssem, rsem, rr, cc):
        return pltpu.make_async_remote_copy(src_ref=src, dst_ref=dst, send_sem=ssem, recv_sem=rsem,
                                            device_id=(rr, cc), device_id_type=MESH)

    def to_left(k, p):
        return remote(tile[k].at[0, p], tile[k].at[1, p], fs.at[0, k, p], fr.at[0, k, p], r, left)

    def to_up(k, p):
        return remote(tile[k].at[0, p], tile[k].at[2, p], fs.at[1, k, p], fr.at[1, k, p], up, c)

    def pass_up(k, p):
        return remote(tile[k].at[1, p], tile[k].at[3, p], fs.at[2, k, p], fr.at[2, k, p], up, c)

    for k in range(4):
        for p in range(2):
            ins[2 * k + p].wait()
            for m in range(4):
                tile[k][0, p, m] = objn[p, k, pl.ds(m, QUARTER, stride=4), :].astype(BF)
            if k == 0 and p == 0:
                pl.semaphore_wait(barrier, 4)
            to_left(k, p).start()
            to_up(k, p).start()
    for copy in ins[8:]:
        copy.wait()

    total = jnp.zeros((8, SIDE), F32)
    for p in range(2):
        def add(i, acc, p=p):
            x = jnp.concatenate([prbn[p, k, pl.ds(pl.multiple_of(i * 8, 8), 8), :] for k in range(4)], axis=1)
            return acc + x * x
        total = lax.fori_loop(0, SIDE // 8, add, total)
    mean = jnp.sum(jnp.sum(total, axis=1, keepdims=True), axis=0, keepdims=True) * (1.0 / (SIDE * SIDE)) + EPS
    power[...] = jnp.broadcast_to(STEP / mean, (8, QUARTER))

    def prepare(s):
        oy, ox = offy[0, s], offx[0, s]
        live = jnp.where(s < cnt[0, 0], 1.0, 0.0).astype(F32)
        lam, freq = iota((SIDE, SIDE), 1), iota((SIDE, SIDE), 0)
        lane = lam & 127
        even_minus = jnp.where(lane == 0, HALF, SIDE - 2 * lane)
        want = jnp.where(lam < 128, 2 * lane,
                         jnp.where(lam < 256, 2 * lane + 1,
                                   jnp.where(lam < 384, even_minus, SIDE - 1 - 2 * lane)))
        mixed = dot(ampr[s], one_hot(freq == want)).astype(BF)
        pick = one_hot(lam == 4 * (freq & 127) + (freq >> 7))
        ampp[s] = dot(pick, mixed).astype(BF).reshape(4, QUARTER, SIDE)
        for m in range(4):
            turn = lax.shift_right_logical(oy + m, 2) & 127
            for p in range(2):
                x = strided(prbn, p, m, QUARTER) * live
                x = pltpu.roll(pltpu.roll(x, turn, 0), ox, 1)
                for k in range(4):
                    prot[s, k, p, m] = x[:, k * QUARTER:(k + 1) * QUARTER]
            cs = pltpu.roll(b1[:, m * QUARTER:(m + 1) * QUARTER].astype(F32), turn, 1)
            cc, ss = cs[:QUARTER], cs[QUARTER:]
            t1[s, m] = jnp.concatenate([jnp.concatenate([cc, -ss], axis=1),
                                        jnp.concatenate([ss, cc], axis=1)], axis=0).astype(BF)
        rows, cols = iota((SIDE, SIDE), 0), iota((SIDE, SIDE), 1)
        t2[s] = dot(one_hot(cols == ((rows - ox) & 511)), b2[...]).astype(BF)
        rows, cols = iota((SIDE, HALF), 0), iota((SIDE, HALF), 1)
        cs = dot(b3[...], one_hot(rows == ((cols - ox) & 511)))
        for par in range(2):
            a = par * QUARTER
            cc = jnp.concatenate([cs[a:a + 128], cs[a + 256:a + 384]], axis=0)
            ss = jnp.concatenate([cs[a + 512:a + 640], cs[a + 768:a + 896]], axis=0)
            t3[s, par] = jnp.concatenate([jnp.concatenate([cc, -ss], axis=1),
                                          jnp.concatenate([ss, cc], axis=1)], axis=0).astype(BF)
        rows, cols = iota((QUARTER, SIDE), 0), iota((QUARTER, SIDE), 1)
        place = 4 * (rows & 31) + lax.shift_right_logical(rows, 5)
        cs = dot(one_hot(cols == ((place - oy) & 511)), b4[...])
        for m in range(4):
            cc = cs[:, m * QUARTER:(m + 1) * QUARTER]
            ss = cs[:, SIDE + m * QUARTER:SIDE + (m + 1) * QUARTER]
            t4[s, m] = jnp.concatenate([jnp.concatenate([cc, ss], axis=1),
                                        jnp.concatenate([-ss, cc], axis=1)], axis=0).astype(BF)

    def hand_on(k):
        for p in range(2):
            to_left(k, p).wait_recv()
            pass_up(k, p).start()

    def arrived(k):
        for p in range(2):
            to_up(k, p).wait_recv()
        for p in range(2):
            pass_up(k, p).wait_recv()

    def first_stage(k0, nk):
        wide = nk * QUARTER
        cols = slice(k0 * QUARTER, k0 * QUARTER + wide)

        def wider(read):
            return jnp.concatenate([read(k) for k in range(k0, k0 + nk)], axis=1)

        def one(s, carry):
            oy, ox = offy[0, s], offx[0, s]
            for m in range(4):
                mu = (m + oy) & 3
                xs = []
                for i in range(0, QUARTER, 32):
                    rs = slice(i, i + 32)
                    own_row = 4 * (iota((32, wide), 0) + i) + mu >= oy
                    own_col = iota((32, wide), 1) + k0 * QUARTER >= ox
                    part = []
                    for p in range(2):
                        q = [wider(lambda k, j=j: tile[k][j, p, mu, rs, :]).astype(F32) for j in range(4)]
                        part.append(jnp.where(own_row, jnp.where(own_col, q[0], q[1]),
                                              jnp.where(own_col, q[2], q[3])))
                    pr, pi = [wider(lambda k, p=p: prot[s, k, p, m, rs, :]) for p in range(2)]
                    xs.append(((pr * part[0] - pi * part[1]).astype(BF), (pr * part[1] + pi * part[0]).astype(BF)))
                x = jnp.concatenate([a for a, _ in xs] + [b for _, b in xs], axis=0)
                gbuf[m, :, :wide] = dot(t1[s, m], x)
            for i in range(0, QUARTER, 32):
                re, im = slice(i, i + 32), slice(QUARTER + i, QUARTER + i + 32)
                outs = butterfly([(gbuf[m, re, :wide], gbuf[m, im, :wide]) for m in range(4)], -1)
                for q, (xr, xi) in enumerate(outs):
                    hb[s, 0, i // 32, q * 32:(q + 1) * 32, cols] = xr.astype(BF)
                    hb[s, 1, i // 32, q * 32:(q + 1) * 32, cols] = xi.astype(BF)
            return carry

        lax.fori_loop(0, SLOTS, one, 0)

    def prepare_and_pass(s, carry):
        prepare(s)
        for k in range(2):
            @pl.when(s == k)
            def _(k=k):
                hand_on(k)
        return carry

    lax.fori_loop(0, SLOTS, prepare_and_pass, 0)
    hand_on(2)
    arrived(0)
    arrived(1)
    first_stage(0, 2)
    hand_on(3)
    arrived(2)
    first_stage(2, 1)
    arrived(3)
    first_stage(3, 1)

    def middle(s, carry):
        def spectrum(m):
            prod = dot(jnp.concatenate([hb[s, 0, m], hb[s, 1, m]], axis=0), t2[s])
            gtwo[m % 2, 0] = prod[:, :HALF]
            gtwo[m % 2, 1] = prod[:, HALF:]

        spectrum(0)
        for m in range(4):
            if m < 3:
                spectrum(m + 1)
            g, d = gtwo.at[m % 2], dbuf.at[m % 2]
            for i in range(0, QUARTER, 32):
                re, im = slice(i, i + 32), slice(QUARTER + i, QUARTER + i + 32)
                for par in range(2):
                    ln = slice(par * 128, par * 128 + 128)
                    rc, ic = g[0, re, ln], g[0, im, ln]
                    rs_, is_ = g[1, re, ln], g[1, im, ln]
                    pr_, pi_ = rc - is_, ic + rs_
                    mr_, mi_ = rc + is_, ic - rs_
                    if par == 0:
                        first = iota((32, QUARTER), 1) == 0
                        pr_, pi_ = jnp.where(first, rc, pr_), jnp.where(first, ic, pi_)
                        mr_, mi_ = jnp.where(first, rs_, mr_), jnp.where(first, is_, mi_)
                    for k, (a, b) in enumerate([(pr_, pi_), (mr_, mi_)]):
                        tt = 2 * k + par
                        mag = ampp[s, m, i:i + 32, tt * 128:(tt + 1) * 128].astype(F32)
                        factor = mag * lax.rsqrt(jnp.maximum(a * a + b * b, 0.25)) - 1.0
                        d[par, i:i + 32, k * 128:(k + 1) * 128] = (a * factor).astype(BF)
                        d[par, i:i + 32, 256 + k * 128:256 + (k + 1) * 128] = (b * factor).astype(BF)
            e = dot(d[0], t3[s, 0])
            o = dot(d[1], t3[s, 1])
            a, b = e + o, e - o
            hb[s, 0, m, :, :HALF] = a[:, :HALF].astype(BF)
            hb[s, 1, m, :, :HALF] = a[:, HALF:].astype(BF)
            hb[s, 0, m, :, HALF:] = b[:, :HALF].astype(BF)
            hb[s, 1, m, :, HALF:] = b[:, HALF:].astype(BF)
        return carry

    lax.fori_loop(0, SLOTS, middle, 0)

    def down_right(k, j):
        return remote(slr.at[k, j], rlr.at[k, j], bs.at[0, k, j], br.at[0, k, j], down, c)

    def down_left(k, j):
        return remote(sll.at[k, j], rll.at[k, j], bs.at[1, k, j], br.at[1, k, j], down, c)

    def to_right(k, j):
        return remote(sur.at[k, j], rur.at[k, j], bs.at[2, k, j], br.at[2, k, j], r, right)

    def lanes_of(k):
        return pl.ds(pl.multiple_of(k * QUARTER, QUARTER), QUARTER)

    def last_stage(kk, carry):
        k = lax.rem(3 * kk, 4)
        cols = lanes_of(k)

        def one(s, inner):
            oy = offy[0, s]
            for m in range(4):
                x = jnp.concatenate([hb[s, 0, m, :, cols], hb[s, 1, m, :, cols]], axis=0)
                gbuf[m, :, :QUARTER] = dot(t4[s, m], x)
            for i in range(0, QUARTER, 32):
                re, im = slice(i, i + 32), slice(QUARTER + i, QUARTER + i + 32)
                outs = butterfly([(gbuf[m, re, :QUARTER], gbuf[m, im, :QUARTER]) for m in range(4)], 1)
                mu = i // 32
                m = (mu - oy) & 3
                for q, (wr, wi) in enumerate(outs):
                    rs = slice(q * 32, (q + 1) * 32)
                    pr, pi = prot[s, k, 0, m, rs, :], prot[s, k, 1, m, rs, :]
                    term[s, 0, mu, rs, :] = pr * wr + pi * wi
                    term[s, 1, mu, rs, :] = pr * wi - pi * wr
            return inner

        lax.fori_loop(0, SLOTS, one, 0)
        zero = jnp.zeros((32, QUARTER), F32)
        lanes = iota((32, QUARTER), 1) + k * QUARTER
        for at, m in enumerate(ORDER):
            j, n = at // 2, at % 2
            for i in range(0, QUARTER, 32):
                rs = slice(i, i + 32)
                rows = 4 * (iota((32, QUARTER), 0) + i) + m
                for p in range(2):
                    al, ur, ll, lr = zero, zero, zero, zero
                    for s in range(SLOTS):
                        x = term[s, p, m, rs, :]
                        own_row, own_col = rows >= offy[0, s], lanes >= offx[0, s]
                        u = jnp.where(own_row, x, zero)
                        l = jnp.where(own_row, zero, x)
                        al = al + jnp.where(own_col, u, zero)
                        ur = ur + jnp.where(own_col, zero, u)
                        ll = ll + jnp.where(own_col, l, zero)
                        lr = lr + jnp.where(own_col, zero, l)
                    hs[p, m, rs, cols] = al
                    urf[k, j, n, p, rs, :] = ur
                    sll[k, j, n, p, rs, :] = ll.astype(BF)
                    slr[k, j, n, p, rs, :] = lr.astype(BF)
            if at == 1:
                down_right(k, 0).start()

        @pl.when(kk > 0)
        def _():
            add_right(lax.rem(3 * kk + 1, 4), 0)
        return carry

    def add_right(k, j):
        down_right(k, j).wait_recv()
        for n in range(2):
            for p in range(2):
                sur[k, j, n, p] = (urf[k, j, n, p] + rlr[k, j, n, p].astype(F32)).astype(BF)
        to_right(k, j).start()

    lax.fori_loop(0, 4, last_stage, 0)
    for k in BLOCKS:
        down_right(k, 1).start()
    add_right(1, 0)
    for k in BLOCKS:
        down_left(k, 0).start()
    add_right(0, 1)
    add_right(3, 1)
    for k in BLOCKS:
        down_left(k, 1).start()
    add_right(2, 1)
    add_right(1, 1)

    def row_rims(k):
        return [remote(msg.at[2 * k + d], halo.at[2 * k + d], hsem.at[2 * k + d], hrem.at[2 * k + d], rr, c)
                for d, rr in ((0, up), (1, down))]

    def column_rim(k):
        n, cc = (0, left) if k == 0 else (1, right)
        return remote(side.at[n], beside.at[n], hsem.at[8 + n], hrem.at[8 + n], r, cc)

    scale = power[0:1, 0:1]
    for j in range(2):
        for k in BLOCKS:
            cols = slice(k * QUARTER, (k + 1) * QUARTER)
            down_left(k, j).wait_recv()
            to_right(k, j).wait_recv()
            for n in range(2):
                m = ORDER[2 * j + n]
                for p in range(2):
                    for i in range(0, QUARTER, 64):
                        rs = slice(i, i + 64)
                        sums = hs[p, m, rs, cols] + (rll[k, j, n, p, rs, :].astype(F32) + rur[k, j, n, p, rs, :].astype(F32))
                        hs[p, m, rs, cols] = objn[p, k, pl.ds(m + 4 * i, 64, stride=4), :] + scale * sums
            if j == 0:
                for p in range(2):
                    msg[2 * k, p:p + 1, :] = hs[p, 0, 0:1, cols]
                    msg[2 * k + 1, p:p + 1, :] = hs[p, 3, 127:128, cols]
                for copy in row_rims(k):
                    copy.start()
            elif k in (0, 3):
                lane = iota((QUARTER, QUARTER), 1)
                edge = jnp.zeros((QUARTER, QUARTER), F32)
                for at in range(8):
                    turn = at if k == 0 else (at + 1) % QUARTER
                    edge = jnp.where(lane == at, pltpu.roll(hs[at // 4, at % 4, :, cols], turn, 1), edge)
                side[k // 3, 0:8, :] = edge.T[0:8]
                for copy in row_rims(k):
                    copy.wait_recv()
                side[k // 3, 8:16, :] = halo[2 * k]
                side[k // 3, 16:24, :] = halo[2 * k + 1]
                column_rim(k).start()
    for k in (1, 2):
        for copy in row_rims(k):
            copy.wait_recv()
    for k in (0, 3):
        column_rim(k).wait_recv()
    rim[0:8] = halo[...]
    for n in range(2):
        for g in range(3):
            rim[8 + 3 * n + g] = beside[n, 8 * g:8 * g + 8, :]

    for k in range(4):
        for p in range(2):
            for copy in (to_left(k, p), to_up(k, p), pass_up(k, p), down_right(k, p), down_left(k, p), to_right(k, p)):
                copy.wait_send()
        for copy in row_rims(k):
            copy.wait_send()
    for k in (0, 3):
        column_rim(k).wait_send()


def clean_kernel(hs, halo, outr, outi, ext, res, last, outn, colt, outsem):
    filler = jnp.zeros((QUARTER - 8, QUARTER), F32)
    for k in range(2):
        colt[k, 0:QUARTER, :] = jnp.concatenate([halo[8 + 3 * k], filler], axis=0).T

    lane8 = iota((8, QUARTER), 1)
    for k, (src, ln) in enumerate([(9, 0), (12, 127)]):
        row = jnp.zeros((8, QUARTER), F32)
        for p in range(2):
            v = jnp.broadcast_to(halo[src, p:p + 1, :], (8, QUARTER))
            row = jnp.where(lane8 == 4 * p, pltpu.roll(v, (4 * p - ln) % QUARTER, 1), row)
        colt[k, QUARTER:QUARTER + 8, :] = row

    def out_copy(p, k):
        return pltpu.make_async_copy(outn.at[p, k], (outr, outi)[p].at[:, k * QUARTER:(k + 1) * QUARTER], outsem.at[p, k])

    def out_part(p, k, i):
        rs = pl.ds(4 * i - 64, 128)
        return pltpu.make_async_copy(outn.at[p, k, rs], (outr, outi)[p].at[rs, k * QUARTER:(k + 1) * QUARTER], outsem.at[p, k])

    def partner(x, lanes_odd, shifted, xr=None, xl=None):
        ahead, behind = pltpu.roll(x, SIDE - 1, 1), pltpu.roll(x, 1, 1)
        if not shifted:
            return jnp.where(lanes_odd, behind, ahead)
        q = jnp.where(lanes_odd, ahead, behind)
        ln = iota((x.shape[0], QUARTER), 1)
        return jnp.concatenate([jnp.where(ln == 0, xl, q[:, :128]), q[:, 128:384],
                                jnp.where(ln == 127, xr, q[:, 384:])], axis=1)

    def clipped(x):
        return x - jnp.clip(x, -2 * SHRINK, 2 * SHRINK)

    def clean(a, b, shifted, ar=None, br_=None, al=None, bl=None):
        odd = (iota(a.shape, 1) & 1) == 1
        s, d = a + b, a - b
        if shifted:
            ps = partner(s, odd, True, ar + br_, al + bl)
            pd = partner(d, odd, True, ar - br_, al - bl)
        else:
            ps, pd = partner(s, odd, False), partner(d, odd, False)
        x = (s + ps) + clipped(s - ps)
        y = clipped(d + pd) + clipped(d - pd)
        return x + y, x - y

    for p in range(2):
        ext[0:QUARTER, :] = hs[p, 0]
        for k in range(4):
            ext[QUARTER:QUARTER + 1, k * 128:(k + 1) * 128] = halo[2 * k, p:p + 1, :]

        def at_right(rs, m):
            return pltpu.roll(colt[0, rs, :], (127 - (4 * p + m)) % QUARTER, 1)

        def at_left(rs, m):
            return pltpu.roll(colt[1, rs, :], (QUARTER - (4 * p + m)) % QUARTER, 1)

        above = jnp.concatenate([halo[2 * k + 1, p:p + 1, :] for k in range(4)], axis=1)
        corner_l = pltpu.roll(jnp.broadcast_to(halo[13, p:p + 1, :], (8, QUARTER)), 1, 1)
        corner_r = pltpu.roll(jnp.broadcast_to(halo[10, p:p + 1, :], (8, QUARTER)), 127, 1)
        eight = slice(0, 8)
        _, top = clean(jnp.broadcast_to(above, (8, SIDE)), hs[p, 0, eight, :], True,
                       corner_r, at_right(eight, 0), corner_l, at_left(eight, 0))
        res[0:1, :] = top[0:1, :]
        for i in range(0, QUARTER, 16):
            rs, nx = slice(i, i + 16), slice(i + 1, i + 17)
            x, y = clean(hs[p, 3, rs, :], ext[nx, :], True,
                         at_right(rs, 3), at_right(nx, 0), at_left(rs, 3), at_left(nx, 0))
            res[nx, :] = y
            last[rs, :] = x
        for i in range(0, QUARTER, 16):
            rs = slice(i, i + 16)
            x1, x2 = clean(hs[p, 1, rs, :], hs[p, 2, rs, :], True,
                           at_right(rs, 1), at_right(rs, 2), at_left(rs, 1), at_left(rs, 2))
            h0, h1 = clean(hs[p, 0, rs, :], hs[p, 1, rs, :], False)
            h2, h3 = clean(hs[p, 2, rs, :], hs[p, 3, rs, :], False)
            outs = [h0 + res[rs, :], h1 + x1, h2 + x2, h3 + last[rs, :]]
            for m in range(4):
                for k in range(4):
                    outn[p, k, pl.ds(m + 4 * i, 16, stride=4), :] = 0.125 * outs[m][:, k * 128:(k + 1) * 128]
            if i % 32 == 16:
                for k in range(4):
                    out_part(p, k, i).start()
    for p in range(2):
        for k in range(4):
            out_copy(p, k).wait()


def body(obj_re, obj_im, probe_re, probe_im, amplitude, offset_y, offset_x, counts):
    plane = (SIDE, SIDE)
    classes = (4, QUARTER, SIDE)
    square = (QUARTER, QUARTER)
    split = (2, 4, SIDE, QUARTER)
    vm = pltpu.VMEM
    scratch = [
        vm(split, F32), *[vm((4, 2, 4) + square, BF)] * 4, vm(split, F32), vm((SLOTS, 4, 2, 4) + square, F32),
        vm((SLOTS,) + plane, BF), vm((SLOTS,) + classes, BF),
        vm((HALF, SIDE), BF), vm(plane, BF), vm((2 * SIDE, SIDE), BF), vm((SIDE, 2 * SIDE), BF),
        vm((SLOTS, 4, HALF, HALF), BF), vm((SLOTS,) + plane, BF), vm((SLOTS, 2) + plane, BF), vm((SLOTS, 4, HALF, HALF), BF),
        vm((4, HALF, HALF), F32), vm((2, 2, HALF, HALF), F32), vm((SLOTS, 2) + classes, BF), vm((2, 2, QUARTER, SIDE), BF),
        vm((SLOTS, 2, 4) + square, F32),
    ] + [vm((4, 2, 2, 2) + square, BF)] * 6 + [
        vm((4, 2, 2, 2) + square, F32),
        vm((8, 8, QUARTER), F32), vm((8, 8, QUARTER), F32), vm((2, 24, QUARTER), F32), vm((2, 24, QUARTER), F32), vm((8, QUARTER), F32),
        pltpu.SemaphoreType.DMA((21,)),
    ] + [pltpu.SemaphoreType.DMA((3, 4, 2))] * 4 + [pltpu.SemaphoreType.DMA((10,))] * 2
    smem = pl.BlockSpec(memory_space=pltpu.SMEM)
    anyw = pl.BlockSpec(memory_space=pl.ANY)
    onchip = pl.BlockSpec(memory_space=pltpu.VMEM)
    hs, rim = pl.pallas_call(
        kernel,
        out_shape=(pltpu.VMEM((2,) + classes, F32), pltpu.VMEM((14, 8, QUARTER), F32)),
        in_specs=[smem] * 3 + [anyw] * 9,
        out_specs=(onchip, onchip),
        scratch_shapes=scratch,
        compiler_params=pltpu.CompilerParams(collective_id=0, has_side_effects=True, vmem_limit_bytes=60 << 20),
    )(offset_y, offset_x, counts, obj_re, obj_im, probe_re, probe_im, amplitude, *[jnp.asarray(t) for t in tables()])
    return pl.pallas_call(
        clean_kernel,
        out_shape=(jax.ShapeDtypeStruct(plane, F32),) * 2,
        in_specs=[onchip, onchip],
        out_specs=(anyw, anyw),
        scratch_shapes=[vm((QUARTER + 8, SIDE), F32), vm((QUARTER + 8, SIDE), F32), vm((QUARTER, SIDE), F32),
                        vm(split, F32), vm((2, QUARTER + 8, QUARTER), F32), pltpu.SemaphoreType.DMA((2, 4))],
        compiler_params=pltpu.CompilerParams(vmem_limit_bytes=16 << 20),
    )(hs, rim)


def solution(mesh):
    return jax.shard_map(
        body,
        mesh=mesh,
        in_specs=(P("row", "col"), P("row", "col"), P(), P(), P("row", "col", None, None),
                  P("row", "col"), P("row", "col"), P("row", "col")),
        out_specs=(P("row", "col"), P("row", "col")),
        check_vma=False,
    )
```

```python
import math

import jax
import jax.numpy as jnp
import ml_dtypes
import numpy as np
from jax import lax
from jax.experimental import pallas as pl
from jax.experimental.pallas import tpu as pltpu
from jax.sharding import PartitionSpec as P

SIDE = 512
QUARTER = 128
HALF = 256
SLOTS = 4
EPS = 1e-05
STEP = 0.5
SHRINK = 0.2
BF = jnp.bfloat16
F32 = jnp.float32
MESH = pl.DeviceIdType.MESH


def tables():
    phase = np.arange(SIDE) * (2.0 * math.pi / SIDE)
    norming = 1.0 / math.sqrt(SIDE)
    cosine = (np.cos(phase) * norming).astype(np.float32)
    sine = (-np.sin(phase) * norming).astype(np.float32)
    quarter = np.arange(4) * QUARTER
    cosine[quarter[1::2]] = 0.0
    sine[quarter[0::2]] = 0.0

    def entries(rows, cols):
        at = np.outer(rows, cols) % SIDE
        return cosine[at], sine[at]

    natural = np.arange(SIDE)
    by_class = np.concatenate([natural[m::4] for m in range(4)])
    block = np.concatenate([np.arange(m, QUARTER, 4) for m in range(4)])
    even, odd = np.arange(0, HALF, 2), np.arange(1, HALF, 2)
    minus_even = (SIDE - even) % SIDE
    minus_even[0] = HALF
    freq = np.concatenate([even, odd, minus_even, SIDE - odd])
    c, s = entries(block, by_class)
    first = np.concatenate([c, s], axis=0)
    c, s = entries(natural, freq[:HALF])
    s[:, 0] = entries(natural, np.array([HALF]))[0][:, 0]
    second = np.concatenate([c, s], axis=1)
    c, s = entries(freq, natural)
    third = np.concatenate([c, s], axis=0)
    c, s = entries(natural, by_class)
    fourth = np.concatenate([c, s], axis=1)
    return [t.astype(ml_dtypes.bfloat16) for t in (first, second, third, fourth)]


def dot(a, b):
    return jnp.dot(a, b, preferred_element_type=F32)


def iota(shape, dim):
    return lax.broadcasted_iota(jnp.int32, shape, dim)


def strided(ref, p, start, size):
    return jnp.concatenate([ref[p, k, pl.ds(start, size, stride=4), :] for k in range(4)], axis=1)


def one_hot(hit):
    return jnp.where(hit, 1.0, 0.0).astype(BF)


ORDER = (0, 3, 1, 2)
BLOCKS = (0, 3, 2, 1)


def butterfly(g, sign):
    ar, ai = g[0][0] + g[2][0], g[0][1] + g[2][1]
    br, bi = g[0][0] - g[2][0], g[0][1] - g[2][1]
    cr, ci = g[1][0] + g[3][0], g[1][1] + g[3][1]
    dr, di = g[1][0] - g[3][0], g[1][1] - g[3][1]
    one = (br - di, bi + dr)
    three = (br + di, bi - dr)
    if sign < 0:
        one, three = three, one
    return [(ar + cr, ai + ci), one, (ar - cr, ai - ci), three]


def kernel(offy, offx, cnt, objr, obji, prbr, prbi, amp, b1h, b2h, b3h, b4h,
           hs, rim,
           objn, tile0, tile1, tile2, tile3, prbn, prot, ampr, ampp, b1, b2, b3, b4,
           t1, t2, t3, t4, gbuf, gtwo, hb, dbuf, term,
           slr, sur, sll, rlr, rll, rur, urf,
           msg, halo, side, beside, power,
           insem, fs, fr, bs, br, hsem, hrem):
    tile = (tile0, tile1, tile2, tile3)
    nr, nc = lax.axis_size("row"), lax.axis_size("col")
    r, c = lax.axis_index("row"), lax.axis_index("col")
    up, down = lax.rem(r + nr - 1, nr), lax.rem(r + 1, nr)
    left, right = lax.rem(c + nc - 1, nc), lax.rem(c + 1, nc)

    moves = []
    for pair, dst in (((objr, obji), objn), ((prbr, prbi), prbn)):
        moves += [(pair[p].at[:, k * QUARTER:(k + 1) * QUARTER], dst.at[p, k]) for k in range(4) for p in range(2)]
    moves += [(b1h, b1), (amp.at[0], ampr), (b2h, b2), (b3h, b3), (b4h, b4)]
    ins = [pltpu.make_async_copy(a, b, insem.at[i]) for i, (a, b) in enumerate(moves)]
    for copy in ins:
        copy.start()

    barrier = pltpu.get_barrier_semaphore()
    for rr, cc in ((up, c), (down, c), (r, left), (r, right)):
        pl.semaphore_signal(barrier, inc=1, device_id=(rr, cc), device_id_type=MESH)

    def remote(src, dst, ssem, rsem, rr, cc):
        return pltpu.make_async_remote_copy(src_ref=src, dst_ref=dst, send_sem=ssem, recv_sem=rsem,
                                            device_id=(rr, cc), device_id_type=MESH)

    def to_left(k, p):
        return remote(tile[k].at[0, p], tile[k].at[1, p], fs.at[0, k, p], fr.at[0, k, p], r, left)

    def to_up(k, p):
        return remote(tile[k].at[0, p], tile[k].at[2, p], fs.at[1, k, p], fr.at[1, k, p], up, c)

    def pass_up(k, p):
        return remote(tile[k].at[1, p], tile[k].at[3, p], fs.at[2, k, p], fr.at[2, k, p], up, c)

    for k in range(4):
        for p in range(2):
            ins[2 * k + p].wait()
            for m in range(4):
                tile[k][0, p, m] = objn[p, k, pl.ds(m, QUARTER, stride=4), :].astype(BF)
            if k == 0 and p == 0:
                pl.semaphore_wait(barrier, 4)
            to_left(k, p).start()
            to_up(k, p).start()
    for copy in ins[8:]:
        copy.wait()

    total = jnp.zeros((8, SIDE), F32)
    for p in range(2):
        def add(i, acc, p=p):
            x = jnp.concatenate([prbn[p, k, pl.ds(pl.multiple_of(i * 8, 8), 8), :] for k in range(4)], axis=1)
            return acc + x * x
        total = lax.fori_loop(0, SIDE // 8, add, total)
    mean = jnp.sum(jnp.sum(total, axis=1, keepdims=True), axis=0, keepdims=True) * (1.0 / (SIDE * SIDE)) + EPS
    power[...] = jnp.broadcast_to(STEP / mean, (8, QUARTER))

    def prepare(s):
        oy, ox = offy[0, s], offx[0, s]
        live = jnp.where(s < cnt[0, 0], 1.0, 0.0).astype(F32)
        lam, freq = iota((SIDE, SIDE), 1), iota((SIDE, SIDE), 0)
        lane = lam & 127
        even_minus = jnp.where(lane == 0, HALF, SIDE - 2 * lane)
        want = jnp.where(lam < 128, 2 * lane,
                         jnp.where(lam < 256, 2 * lane + 1,
                                   jnp.where(lam < 384, even_minus, SIDE - 1 - 2 * lane)))
        mixed = dot(ampr[s], one_hot(freq == want)).astype(BF)
        pick = one_hot(lam == 4 * (freq & 127) + (freq >> 7))
        ampp[s] = dot(pick, mixed).astype(BF).reshape(4, QUARTER, SIDE)
        for m in range(4):
            turn = lax.shift_right_logical(oy + m, 2) & 127
            for p in range(2):
                x = strided(prbn, p, m, QUARTER) * live
                x = pltpu.roll(pltpu.roll(x, turn, 0), ox, 1)
                for k in range(4):
                    prot[s, k, p, m] = x[:, k * QUARTER:(k + 1) * QUARTER]
            cs = pltpu.roll(b1[:, m * QUARTER:(m + 1) * QUARTER].astype(F32), turn, 1)
            cc, ss = cs[:QUARTER], cs[QUARTER:]
            t1[s, m] = jnp.concatenate([jnp.concatenate([cc, -ss], axis=1),
                                        jnp.concatenate([ss, cc], axis=1)], axis=0).astype(BF)
        rows, cols = iota((SIDE, SIDE), 0), iota((SIDE, SIDE), 1)
        t2[s] = dot(one_hot(cols == ((rows - ox) & 511)), b2[...]).astype(BF)
        rows, cols = iota((SIDE, HALF), 0), iota((SIDE, HALF), 1)
        cs = dot(b3[...], one_hot(rows == ((cols - ox) & 511)))
        for par in range(2):
            a = par * QUARTER
            cc = jnp.concatenate([cs[a:a + 128], cs[a + 256:a + 384]], axis=0)
            ss = jnp.concatenate([cs[a + 512:a + 640], cs[a + 768:a + 896]], axis=0)
            t3[s, par] = jnp.concatenate([jnp.concatenate([cc, -ss], axis=1),
                                          jnp.concatenate([ss, cc], axis=1)], axis=0).astype(BF)
        rows, cols = iota((QUARTER, SIDE), 0), iota((QUARTER, SIDE), 1)
        place = 4 * (rows & 31) + lax.shift_right_logical(rows, 5)
        cs = dot(one_hot(cols == ((place - oy) & 511)), b4[...])
        for m in range(4):
            cc = cs[:, m * QUARTER:(m + 1) * QUARTER]
            ss = cs[:, SIDE + m * QUARTER:SIDE + (m + 1) * QUARTER]
            t4[s, m] = jnp.concatenate([jnp.concatenate([cc, ss], axis=1),
                                        jnp.concatenate([-ss, cc], axis=1)], axis=0).astype(BF)

    def hand_on(k):
        for p in range(2):
            to_left(k, p).wait_recv()
            pass_up(k, p).start()

    def arrived(k):
        for p in range(2):
            to_up(k, p).wait_recv()
        for p in range(2):
            pass_up(k, p).wait_recv()

    def first_stage(k0, nk):
        wide = nk * QUARTER
        cols = slice(k0 * QUARTER, k0 * QUARTER + wide)

        def wider(read):
            return jnp.concatenate([read(k) for k in range(k0, k0 + nk)], axis=1)

        def one(s, carry):
            oy, ox = offy[0, s], offx[0, s]
            for m in range(4):
                mu = (m + oy) & 3
                xs = []
                for i in range(0, QUARTER, 32):
                    rs = slice(i, i + 32)
                    own_row = 4 * (iota((32, wide), 0) + i) + mu >= oy
                    own_col = iota((32, wide), 1) + k0 * QUARTER >= ox
                    part = []
                    for p in range(2):
                        q = [wider(lambda k, j=j: tile[k][j, p, mu, rs, :]) for j in range(4)]
                        part.append(jnp.where(own_row, jnp.where(own_col, q[0], q[1]),
                                              jnp.where(own_col, q[2], q[3])).astype(F32))
                    pr, pi = [wider(lambda k, p=p: prot[s, k, p, m, rs, :]) for p in range(2)]
                    xs.append(((pr * part[0] - pi * part[1]).astype(BF), (pr * part[1] + pi * part[0]).astype(BF)))
                x = jnp.concatenate([a for a, _ in xs] + [b for _, b in xs], axis=0)
                gbuf[m, :, :wide] = dot(t1[s, m], x)
            for i in range(0, QUARTER, 32):
                re, im = slice(i, i + 32), slice(QUARTER + i, QUARTER + i + 32)
                outs = butterfly([(gbuf[m, re, :wide], gbuf[m, im, :wide]) for m in range(4)], -1)
                for q, (xr, xi) in enumerate(outs):
                    hb[s, 0, i // 32, q * 32:(q + 1) * 32, cols] = xr.astype(BF)
                    hb[s, 1, i // 32, q * 32:(q + 1) * 32, cols] = xi.astype(BF)
            return carry

        lax.fori_loop(0, SLOTS, one, 0)

    def prepare_and_pass(s, carry):
        prepare(s)
        for k in range(2):
            @pl.when(s == k)
            def _(k=k):
                hand_on(k)
        return carry

    lax.fori_loop(0, SLOTS, prepare_and_pass, 0)
    hand_on(2)
    arrived(0)
    arrived(1)
    first_stage(0, 2)
    hand_on(3)
    arrived(2)
    first_stage(2, 1)
    arrived(3)
    first_stage(3, 1)

    def middle(s, carry):
        def spectrum(m):
            prod = dot(jnp.concatenate([hb[s, 0, m], hb[s, 1, m]], axis=0), t2[s])
            gtwo[m % 2, 0] = prod[:, :HALF]
            gtwo[m % 2, 1] = prod[:, HALF:]

        spectrum(0)
        for m in range(4):
            if m < 3:
                spectrum(m + 1)
            g, d = gtwo.at[m % 2], dbuf.at[m % 2]
            for i in range(0, QUARTER, 32):
                re, im = slice(i, i + 32), slice(QUARTER + i, QUARTER + i + 32)
                for par in range(2):
                    ln = slice(par * 128, par * 128 + 128)
                    rc, ic = g[0, re, ln], g[0, im, ln]
                    rs_, is_ = g[1, re, ln], g[1, im, ln]
                    pr_, pi_ = rc - is_, ic + rs_
                    mr_, mi_ = rc + is_, ic - rs_
                    if par == 0:
                        first = iota((32, QUARTER), 1) == 0
                        pr_, pi_ = jnp.where(first, rc, pr_), jnp.where(first, ic, pi_)
                        mr_, mi_ = jnp.where(first, rs_, mr_), jnp.where(first, is_, mi_)
                    for k, (a, b) in enumerate([(pr_, pi_), (mr_, mi_)]):
                        tt = 2 * k + par
                        mag = ampp[s, m, i:i + 32, tt * 128:(tt + 1) * 128].astype(F32)
                        factor = mag * lax.rsqrt(jnp.maximum(a * a + b * b, 0.25)) - 1.0
                        d[par, i:i + 32, k * 128:(k + 1) * 128] = (a * factor).astype(BF)
                        d[par, i:i + 32, 256 + k * 128:256 + (k + 1) * 128] = (b * factor).astype(BF)
            e = dot(d[0], t3[s, 0])
            o = dot(d[1], t3[s, 1])
            a, b = e + o, e - o
            hb[s, 0, m, :, :HALF] = a[:, :HALF].astype(BF)
            hb[s, 1, m, :, :HALF] = a[:, HALF:].astype(BF)
            hb[s, 0, m, :, HALF:] = b[:, :HALF].astype(BF)
            hb[s, 1, m, :, HALF:] = b[:, HALF:].astype(BF)
        return carry

    lax.fori_loop(0, SLOTS, middle, 0)

    def down_right(k, j):
        return remote(slr.at[k, j], rlr.at[k, j], bs.at[0, k, j], br.at[0, k, j], down, c)

    def down_left(k, j):
        return remote(sll.at[k, j], rll.at[k, j], bs.at[1, k, j], br.at[1, k, j], down, c)

    def to_right(k, j):
        return remote(sur.at[k, j], rur.at[k, j], bs.at[2, k, j], br.at[2, k, j], r, right)

    def lanes_of(k):
        return pl.ds(pl.multiple_of(k * QUARTER, QUARTER), QUARTER)

    def last_stage(kk, carry):
        k = lax.rem(3 * kk, 4)
        cols = lanes_of(k)

        def one(s, inner):
            oy = offy[0, s]
            for m in range(4):
                x = jnp.concatenate([hb[s, 0, m, :, cols], hb[s, 1, m, :, cols]], axis=0)
                gbuf[m, :, :QUARTER] = dot(t4[s, m], x)
            for i in range(0, QUARTER, 32):
                re, im = slice(i, i + 32), slice(QUARTER + i, QUARTER + i + 32)
                outs = butterfly([(gbuf[m, re, :QUARTER], gbuf[m, im, :QUARTER]) for m in range(4)], 1)
                mu = i // 32
                m = (mu - oy) & 3
                for q, (wr, wi) in enumerate(outs):
                    rs = slice(q * 32, (q + 1) * 32)
                    pr, pi = prot[s, k, 0, m, rs, :], prot[s, k, 1, m, rs, :]
                    term[s, 0, mu, rs, :] = pr * wr + pi * wi
                    term[s, 1, mu, rs, :] = pr * wi - pi * wr
            return inner

        lax.fori_loop(0, SLOTS, one, 0)
        zero = jnp.zeros((32, QUARTER), F32)
        lanes = iota((32, QUARTER), 1) + k * QUARTER
        for at, m in enumerate(ORDER):
            j, n = at // 2, at % 2
            for i in range(0, QUARTER, 32):
                rs = slice(i, i + 32)
                rows = 4 * (iota((32, QUARTER), 0) + i) + m
                for p in range(2):
                    al, ur, ll, lr = zero, zero, zero, zero
                    for s in range(SLOTS):
                        x = term[s, p, m, rs, :]
                        own_row, own_col = rows >= offy[0, s], lanes >= offx[0, s]
                        u = jnp.where(own_row, x, zero)
                        l = jnp.where(own_row, zero, x)
                        al = al + jnp.where(own_col, u, zero)
                        ur = ur + jnp.where(own_col, zero, u)
                        ll = ll + jnp.where(own_col, l, zero)
                        lr = lr + jnp.where(own_col, zero, l)
                    hs[p, m, rs, cols] = al
                    urf[k, j, n, p, rs, :] = ur
                    sll[k, j, n, p, rs, :] = ll.astype(BF)
                    slr[k, j, n, p, rs, :] = lr.astype(BF)
            if at == 1:
                down_right(k, 0).start()

        @pl.when(kk > 0)
        def _():
            add_right(lax.rem(3 * kk + 1, 4), 0)
        return carry

    def add_right(k, j):
        down_right(k, j).wait_recv()
        for n in range(2):
            for p in range(2):
                sur[k, j, n, p] = (urf[k, j, n, p] + rlr[k, j, n, p].astype(F32)).astype(BF)
        to_right(k, j).start()

    lax.fori_loop(0, 4, last_stage, 0)
    for k in BLOCKS:
        down_right(k, 1).start()
    add_right(1, 0)
    for k in BLOCKS:
        down_left(k, 0).start()
    add_right(0, 1)
    add_right(3, 1)
    for k in BLOCKS:
        down_left(k, 1).start()
    add_right(2, 1)
    add_right(1, 1)
    for k in range(4):
        for p in range(2):
            for copy in (to_left(k, p), to_up(k, p), pass_up(k, p), down_right(k, p)):
                copy.wait_send()

    def row_rims(k):
        return [remote(msg.at[2 * k + d], halo.at[2 * k + d], hsem.at[2 * k + d], hrem.at[2 * k + d], rr, c)
                for d, rr in ((0, up), (1, down))]

    def column_rim(k):
        n, cc = (0, left) if k == 0 else (1, right)
        return remote(side.at[n], beside.at[n], hsem.at[8 + n], hrem.at[8 + n], r, cc)

    scale = power[0:1, 0:1]
    for j in range(2):
        for k in BLOCKS:
            cols = slice(k * QUARTER, (k + 1) * QUARTER)
            down_left(k, j).wait_recv()
            to_right(k, j).wait_recv()
            for n in range(2):
                m = ORDER[2 * j + n]
                for p in range(2):
                    for i in range(0, QUARTER, 64):
                        rs = slice(i, i + 64)
                        sums = hs[p, m, rs, cols] + (rll[k, j, n, p, rs, :].astype(F32) + rur[k, j, n, p, rs, :].astype(F32))
                        hs[p, m, rs, cols] = objn[p, k, pl.ds(m + 4 * i, 64, stride=4), :] + scale * sums
            if j == 0:
                for p in range(2):
                    msg[2 * k, p:p + 1, :] = hs[p, 0, 0:1, cols]
                    msg[2 * k + 1, p:p + 1, :] = hs[p, 3, 127:128, cols]
                for copy in row_rims(k):
                    copy.start()
            elif k in (0, 3):
                lane = iota((QUARTER, QUARTER), 1)
                edge = jnp.zeros((QUARTER, QUARTER), F32)
                for at in range(8):
                    turn = at if k == 0 else (at + 1) % QUARTER
                    edge = jnp.where(lane == at, pltpu.roll(hs[at // 4, at % 4, :, cols], turn, 1), edge)
                side[k // 3, 0:8, :] = edge.T[0:8]
                for copy in row_rims(k):
                    copy.wait_recv()
                side[k // 3, 8:16, :] = halo[2 * k]
                side[k // 3, 16:24, :] = halo[2 * k + 1]
                column_rim(k).start()
    for k in (1, 2):
        for copy in row_rims(k):
            copy.wait_recv()
    for k in (0, 3):
        column_rim(k).wait_recv()
    rim[0:8] = halo[...]
    rim[8:14] = beside[...].reshape(6, 8, QUARTER)

    for k in range(4):
        for p in range(2):
            down_left(k, p).wait_send()
            to_right(k, p).wait_send()
        for copy in row_rims(k):
            copy.wait_send()
    for k in (0, 3):
        column_rim(k).wait_send()


def clean_kernel(hs, halo, outr, outi, ext, res, last, outn, colt, outsem):
    filler = jnp.zeros((QUARTER - 8, QUARTER), F32)
    for k in range(2):
        colt[k, 0:QUARTER, :] = jnp.concatenate([halo[8 + 3 * k], filler], axis=0).T

    lane8 = iota((8, QUARTER), 1)
    for k, (src, ln) in enumerate([(9, 0), (12, 127)]):
        row = jnp.zeros((8, QUARTER), F32)
        for p in range(2):
            v = jnp.broadcast_to(halo[src, p:p + 1, :], (8, QUARTER))
            row = jnp.where(lane8 == 4 * p, pltpu.roll(v, (4 * p - ln) % QUARTER, 1), row)
        colt[k, QUARTER:QUARTER + 8, :] = row

    def out_copy(p, k):
        return pltpu.make_async_copy(outn.at[p, k], (outr, outi)[p].at[:, k * QUARTER:(k + 1) * QUARTER], outsem.at[p, k])

    def out_part(p, k, i):
        rs = pl.ds(4 * i - 64, 128)
        return pltpu.make_async_copy(outn.at[p, k, rs], (outr, outi)[p].at[rs, k * QUARTER:(k + 1) * QUARTER], outsem.at[p, k])

    def partner(x, lanes_odd, shifted, xr=None, xl=None):
        ahead, behind = pltpu.roll(x, SIDE - 1, 1), pltpu.roll(x, 1, 1)
        if not shifted:
            return jnp.where(lanes_odd, behind, ahead)
        q = jnp.where(lanes_odd, ahead, behind)
        ln = iota((x.shape[0], QUARTER), 1)
        return jnp.concatenate([jnp.where(ln == 0, xl, q[:, :128]), q[:, 128:384],
                                jnp.where(ln == 127, xr, q[:, 384:])], axis=1)

    def clipped(x):
        return x - jnp.clip(x, -2 * SHRINK, 2 * SHRINK)

    def clean(a, b, shifted, ar=None, br_=None, al=None, bl=None):
        odd = (iota(a.shape, 1) & 1) == 1
        s, d = a + b, a - b
        if shifted:
            ps = partner(s, odd, True, ar + br_, al + bl)
            pd = partner(d, odd, True, ar - br_, al - bl)
        else:
            ps, pd = partner(s, odd, False), partner(d, odd, False)
        x = (s + ps) + clipped(s - ps)
        y = clipped(d + pd) + clipped(d - pd)
        return x + y, x - y

    for p in range(2):
        ext[0:QUARTER, :] = hs[p, 0]
        for k in range(4):
            ext[QUARTER:QUARTER + 1, k * 128:(k + 1) * 128] = halo[2 * k, p:p + 1, :]

        def at_right(rs, m):
            return pltpu.roll(colt[0, rs, :], (127 - (4 * p + m)) % QUARTER, 1)

        def at_left(rs, m):
            return pltpu.roll(colt[1, rs, :], (QUARTER - (4 * p + m)) % QUARTER, 1)

        above = jnp.concatenate([halo[2 * k + 1, p:p + 1, :] for k in range(4)], axis=1)
        corner_l = pltpu.roll(jnp.broadcast_to(halo[13, p:p + 1, :], (8, QUARTER)), 1, 1)
        corner_r = pltpu.roll(jnp.broadcast_to(halo[10, p:p + 1, :], (8, QUARTER)), 127, 1)
        eight = slice(0, 8)
        _, top = clean(jnp.broadcast_to(above, (8, SIDE)), hs[p, 0, eight, :], True,
                       corner_r, at_right(eight, 0), corner_l, at_left(eight, 0))
        res[0:1, :] = top[0:1, :]
        for i in range(0, QUARTER, 16):
            rs, nx = slice(i, i + 16), slice(i + 1, i + 17)
            x, y = clean(hs[p, 3, rs, :], ext[nx, :], True,
                         at_right(rs, 3), at_right(nx, 0), at_left(rs, 3), at_left(nx, 0))
            res[nx, :] = y
            last[rs, :] = x
        for i in range(0, QUARTER, 16):
            rs = slice(i, i + 16)
            x1, x2 = clean(hs[p, 1, rs, :], hs[p, 2, rs, :], True,
                           at_right(rs, 1), at_right(rs, 2), at_left(rs, 1), at_left(rs, 2))
            h0, h1 = clean(hs[p, 0, rs, :], hs[p, 1, rs, :], False)
            h2, h3 = clean(hs[p, 2, rs, :], hs[p, 3, rs, :], False)
            outs = [h0 + res[rs, :], h1 + x1, h2 + x2, h3 + last[rs, :]]
            for m in range(4):
                for k in range(4):
                    outn[p, k, pl.ds(m + 4 * i, 16, stride=4), :] = 0.125 * outs[m][:, k * 128:(k + 1) * 128]
            if i % 32 == 16:
                for k in range(4):
                    out_part(p, k, i).start()
    for p in range(2):
        for k in range(4):
            out_copy(p, k).wait()


def body(obj_re, obj_im, probe_re, probe_im, amplitude, offset_y, offset_x, counts):
    plane = (SIDE, SIDE)
    classes = (4, QUARTER, SIDE)
    square = (QUARTER, QUARTER)
    split = (2, 4, SIDE, QUARTER)
    vm = pltpu.VMEM
    scratch = [
        vm(split, F32), *[vm((4, 2, 4) + square, BF)] * 4, vm(split, F32), vm((SLOTS, 4, 2, 4) + square, F32),
        vm((SLOTS,) + plane, BF), vm((SLOTS,) + classes, BF),
        vm((HALF, SIDE), BF), vm(plane, BF), vm((2 * SIDE, SIDE), BF), vm((SIDE, 2 * SIDE), BF),
        vm((SLOTS, 4, HALF, HALF), BF), vm((SLOTS,) + plane, BF), vm((SLOTS, 2) + plane, BF), vm((SLOTS, 4, HALF, HALF), BF),
        vm((4, HALF, HALF), F32), vm((2, 2, HALF, HALF), F32), vm((SLOTS, 2) + classes, BF), vm((2, 2, QUARTER, SIDE), BF),
        vm((SLOTS, 2, 4) + square, F32),
    ] + [vm((4, 2, 2, 2) + square, BF)] * 6 + [
        vm((4, 2, 2, 2) + square, F32),
        vm((8, 8, QUARTER), F32), vm((8, 8, QUARTER), F32), vm((2, 24, QUARTER), F32), vm((2, 24, QUARTER), F32), vm((8, QUARTER), F32),
        pltpu.SemaphoreType.DMA((21,)),
    ] + [pltpu.SemaphoreType.DMA((3, 4, 2))] * 4 + [pltpu.SemaphoreType.DMA((10,))] * 2
    smem = pl.BlockSpec(memory_space=pltpu.SMEM)
    anyw = pl.BlockSpec(memory_space=pl.ANY)
    onchip = pl.BlockSpec(memory_space=pltpu.VMEM)
    hs, rim = pl.pallas_call(
        kernel,
        out_shape=(pltpu.VMEM((2,) + classes, F32), pltpu.VMEM((14, 8, QUARTER), F32)),
        in_specs=[smem] * 3 + [anyw] * 9,
        out_specs=(onchip, onchip),
        scratch_shapes=scratch,
        compiler_params=pltpu.CompilerParams(collective_id=0, has_side_effects=True, vmem_limit_bytes=60 << 20),
    )(offset_y, offset_x, counts, obj_re, obj_im, probe_re, probe_im, amplitude, *[jnp.asarray(t) for t in tables()])
    return pl.pallas_call(
        clean_kernel,
        out_shape=(jax.ShapeDtypeStruct(plane, F32),) * 2,
        in_specs=[onchip, onchip],
        out_specs=(anyw, anyw),
        scratch_shapes=[vm((QUARTER + 8, SIDE), F32), vm((QUARTER + 8, SIDE), F32), vm((QUARTER, SIDE), F32),
                        vm(split, F32), vm((2, QUARTER + 8, QUARTER), F32), pltpu.SemaphoreType.DMA((2, 4))],
        compiler_params=pltpu.CompilerParams(vmem_limit_bytes=16 << 20),
    )(hs, rim)


def solution(mesh):
    return jax.shard_map(
        body,
        mesh=mesh,
        in_specs=(P("row", "col"), P("row", "col"), P(), P(), P("row", "col", None, None),
                  P("row", "col"), P("row", "col"), P("row", "col")),
        out_specs=(P("row", "col"), P("row", "col")),
        check_vma=False,
    )
```
